32 devices in a mesh: gx: 8 (over y, x, core), gy: 4 (over z).
Axes of the slice: x: 2, y: 2, z: 4, core: 2. Of those that a mesh axis runs over, the one named last changes fastest.
Arguments:
- species_field: float32 [168, 156, 672], P('gx', 'gy'), as said below
- start_block: float32 [672, 128], replicated, may hold values from -6 to 6
- trunc_ranks: int32 [3], replicated, may hold values from 64 to 128, as said below
Outputs:
- core_field: float32 [128, 156, 168], P('gx', 'gy')
- energies: float32 [128], replicated
The draws below stay inside these ranges and needn't reach their ends.
Inputs may be any that keep to these rules, and one draw needn't show every extreme that they name: `trunc_ranks`: entry 0 is the rank used in this mode step; one of the three entries equals 128. `species_field`: finite values.
All inputs are finite; a program needn't handle non-finite values.
Results may differ from the reference program's by a relative error of at most 0.00045.
Values sent between devices are 32-bit elements; how exact they have to be, the bound alone decides.
No kernel may reach another device: no remote copies, remote signals or barrier semaphores. Data moves between devices by JAX's collectives and lax.ppermute only.
A program may use at most 64 MiB of HBM per device.

```python
import jax
import jax.numpy as jnp
from jax import lax

I1 = 672
RMAX = 128
ITERS = 3
N2 = 168
N3 = 156


def draw_species_field(key, part):
    keys = jax.random.split(jax.random.fold_in(key, 11), 4)
    row_scale = jnp.exp(jax.random.uniform(keys[0], (1, 1, I1), jnp.float32, 0.0, jnp.log(2.0)))
    slab_scale = jnp.exp(jax.random.uniform(keys[1], (N2, 1, I1), jnp.float32, 0.0, jnp.log(1.6)))
    depth_scale = jnp.exp(jax.random.uniform(keys[2], (1, N3, 1), jnp.float32, 0.0, jnp.log(4.0)))
    ramp = 1.0 + 2.0 * jnp.arange(N2, dtype=jnp.float32).reshape(N2, 1, 1) / (N2 - 1)
    noise = jax.random.normal(keys[3], (N2, N3, I1), jnp.float32)
    return row_scale * slab_scale * depth_scale * ramp * noise


def draw_trunc_ranks(key, part):
    keys = jax.random.split(jax.random.fold_in(key, 23), 2)
    widest = jax.random.randint(keys[0], (), 0, 3)
    others = jax.random.randint(keys[1], (3,), RMAX // 2, RMAX + 1)
    return jnp.where(jnp.arange(3) == widest, RMAX, others).astype(jnp.int32)


def centred(own_key, dims, deviation, limit, kind=jnp.bfloat16):
    return jnp.clip(deviation * jax.random.normal(own_key, dims, jnp.float32), -limit, limit).astype(kind)


def setup_inputs(seed: int = 0) -> dict:
    arg_keys = jax.random.split(jax.random.key(seed), 4)
    return {
        "species_field": draw_species_field(jax.random.fold_in(arg_keys[3], 71), 0),
        "start_block": centred(arg_keys[1], (I1, RMAX), 1.0, 6.0, jnp.float32),
        "trunc_ranks": draw_trunc_ranks(jax.random.fold_in(arg_keys[3], 71), 0),
    }


def orthonormal(columns):
    cross_gram = lax.dot_general(columns, columns, (((0,), (0,)), ((), ())), precision=lax.Precision.HIGHEST)
    factor = jnp.linalg.cholesky(cross_gram)
    return jax.scipy.linalg.solve_triangular(factor, columns.T, lower=True).T

def reference(species_field, start_block, trunc_ranks):
    unfolded = species_field.reshape(-1, I1)
    gram = lax.dot_general(unfolded, unfolded, (((0,), (0,)), ((), ())), precision=lax.Precision.HIGHEST)
    subspace = start_block
    for iteration in range(ITERS):
        images = jnp.dot(gram, subspace, precision=lax.Precision.HIGHEST)
        subspace = orthonormal(images)
    keep_cols = (jnp.arange(RMAX) < trunc_ranks[0]).astype(jnp.float32)
    masked = subspace * keep_cols[None, :]
    core_field = jnp.einsum('bci,ik->kcb', species_field, masked, precision=lax.Precision.HIGHEST)
    caught = jnp.sum(masked * jnp.dot(gram, masked, precision=lax.Precision.HIGHEST), axis=0)
    energies = caught / (jnp.trace(gram) / I1)
    return (core_field, energies)
```

```python
import functools

import jax
import jax.numpy as jnp
from jax import lax
from jax.experimental import pallas as pl
from jax.experimental.pallas import tpu as pltpu
from jax.sharding import PartitionSpec as P

ITERS = 3
LANES = 128
HIGHEST = lax.Precision.HIGHEST
F32 = jnp.float32
BF16 = jnp.bfloat16


def split(value):
    high = value.astype(BF16)
    return high, (value - high.astype(F32)).astype(BF16)


def dot(left, right, left_dim=1, right_dim=0, precision=None):
    return lax.dot_general(
        left,
        right,
        (((left_dim,), (right_dim,)), ((), ())),
        precision=precision,
        preferred_element_type=F32,
    )


def packed_blocks(order):
    full, rest = divmod(order, LANES)
    blocks, row = {}, 0
    for i in range(full):
        for j in range(i, full):
            blocks[i, j] = row
            row += LANES
    if rest:
        for j in range(full + 1):
            blocks[full, j] = row
            row += rest
    return blocks, row


def gram_kernel(x_ref, out_ref, flat, high, low):
    slabs, rows, order = x_ref.shape
    pitch = -(-rows // 8) * 8
    for b in range(slabs):
        flat[pl.ds(b * pitch, rows), :] = x_ref[b]
        if pitch > rows:
            flat[pl.ds(b * pitch + rows, pitch - rows), :] = jnp.zeros((pitch - rows, order), F32)
    spare = flat.shape[0] - slabs * pitch
    if spare:
        flat[pl.ds(slabs * pitch, spare), :] = jnp.zeros((spare, order), F32)
    h, l = split(flat[...])
    high[...] = h
    low[...] = l
    full, rest = divmod(order, LANES)
    blocks, _ = packed_blocks(order)
    for i in range(full):
        rows_i = slice(i * LANES, (i + 1) * LANES)
        cols = slice(i * LANES, full * LANES)
        product = (
            dot(high[:, rows_i], high[:, cols], 0, 0)
            + dot(high[:, rows_i], low[:, cols], 0, 0)
            + dot(low[:, rows_i], high[:, cols], 0, 0)
        )
        for j in range(i, full):
            out_ref[pl.ds(blocks[i, j], LANES), :] = product[:, (j - i) * LANES : (j - i + 1) * LANES]
    if rest:
        rows_i = slice(full * LANES, order)
        product = (
            dot(high[:, rows_i], high[...], 0, 0)
            + dot(high[:, rows_i], low[...], 0, 0)
            + dot(low[:, rows_i], high[...], 0, 0)
        )
        for j in range(full):
            out_ref[pl.ds(blocks[full, j], rest), :] = product[:, j * LANES : (j + 1) * LANES]
        corner = product[:, full * LANES :]
        out_ref[pl.ds(blocks[full, full], rest), :] = jnp.concatenate(
            [corner, jnp.zeros((rest, LANES - rest), F32)], axis=1
        )


def gram_blocks(x):
    slabs, rows, order = x.shape
    depth = -(-slabs * (-(-rows // 8) * 8) // 16) * 16
    _, packed = packed_blocks(order)
    return pl.pallas_call(
        gram_kernel,
        out_shape=jax.ShapeDtypeStruct((packed, LANES), F32),
        scratch_shapes=[
            pltpu.VMEM((depth, order), F32),
            pltpu.VMEM((depth, order), BF16),
            pltpu.VMEM((depth, order), BF16),
        ],
        compiler_params=pltpu.CompilerParams(vmem_limit_bytes=32 << 20),
        name="gram",
    )(x)


def all_sum(value, sizes):
    count_x, count_y = sizes
    ix, iy = lax.axis_index("gx"), lax.axis_index("gy")
    colour = ix & 1
    bits_x = [1 << b for b in range(count_x.bit_length() - 1)]
    bits_y = [1 << b for b in range(count_y.bit_length() - 1)]
    stages_x = list(zip(bits_x[:1], bits_x[:1])) + list(zip(bits_x[1:], reversed(bits_x[1:])))
    stages_y = list(zip(bits_y, reversed(bits_y)))

    def swap(data, flip_x, flip_y):
        pairs = []
        for i in range(count_x):
            for j in range(count_y):
                other = (i ^ flip_x[i & 1]) * count_y + (j ^ flip_y[i & 1])
                pairs.append((i * count_y + j, other))
        return lax.ppermute(data, ("gx", "gy"), pairs)

    for flip in stages_x:
        half = value.shape[0] // 2
        upper = (ix & jnp.where(colour == 0, flip[0], flip[1])) != 0
        keep = jnp.where(upper, half, 0)
        send = lax.dynamic_slice(value, (half - keep, 0), (half, value.shape[1]))
        kept = lax.dynamic_slice(value, (keep, 0), (half, value.shape[1]))
        value = kept + swap(send, flip, (0, 0))
    for flip in stages_y:
        value = value + swap(value, (0, 0), flip)
    for flip in reversed(stages_x):
        upper = (ix & jnp.where(colour == 0, flip[0], flip[1])) != 0
        other = swap(value, flip, (0, 0))
        value = jnp.concatenate([jnp.where(upper, other, value), jnp.where(upper, value, other)], axis=0)
    return value


def eliminate(scaled):
    size = scaled.shape[0]
    lane = lax.broadcasted_iota(jnp.int32, (1, size), 1)
    sub = lax.broadcasted_iota(jnp.int32, (8, 1), 0)
    blocks = [scaled[8 * i : 8 * i + 8, :] for i in range(size // 8)]
    for j in range(size):
        own, at = divmod(j, 8)
        row = blocks[own][at : at + 1, :]
        pivot = (row + jnp.where(lane == j, 1.0, 0.0)) * (1.0 / row[:, j : j + 1])
        for b in range(own, size // 8):
            column = blocks[b][:, j : j + 1]
            if b == own:
                if at == 7:
                    continue
                column = jnp.where(sub > at, column, 0.0)
            blocks[b] = blocks[b] - column * pivot
    return jnp.concatenate(blocks, axis=0)


def orthonormal(columns):
    size = columns.shape[1]
    i = lax.broadcasted_iota(jnp.int32, (size, size), 0)
    j = lax.broadcasted_iota(jnp.int32, (size, size), 1)
    cross_gram = dot(columns, columns, 0, 0, HIGHEST)
    diagonal = jnp.where(i == j, cross_gram, 0.0)
    scale_row = lax.rsqrt(jnp.sum(diagonal, axis=0, keepdims=True))
    scale_col = lax.rsqrt(jnp.sum(diagonal, axis=1, keepdims=True))
    done = eliminate(cross_gram * scale_row * scale_col)
    pivots = jnp.sum(jnp.where(i == j, done, 0.0), axis=1, keepdims=True)
    unit = jnp.where(i > j, done, jnp.where(i == j, 1.0, 0.0))
    inverse = unit * lax.rsqrt(pivots) * scale_row
    return dot(columns, inverse, 1, 1, HIGHEST)


def subspace_kernel(ranks_ref, packed_ref, start_ref, xh_ref, xl_ref, core_ref, energy_ref, gram_high, gram_low, basis):
    order, size = start_ref.shape
    blocks, _ = packed_blocks(order)
    full, rest = divmod(order, LANES)

    trace = jnp.zeros((1, 1), F32)
    for (i, j), row in blocks.items():
        height = LANES if i < full else rest
        width = LANES if j < full else rest
        block = packed_ref[pl.ds(row, height), :][:, :width]
        if i == j:
            a = lax.broadcasted_iota(jnp.int32, (height, width), 0)
            b = lax.broadcasted_iota(jnp.int32, (height, width), 1)
            trace = trace + jnp.sum(jnp.where(a == b, block, 0.0), keepdims=True)
        h, l = split(block)
        gram_high[i * LANES : i * LANES + height, j * LANES : j * LANES + width] = h
        gram_low[i * LANES : i * LANES + height, j * LANES : j * LANES + width] = l
        if i != j:
            h, l = split(block.T)
            gram_high[j * LANES : j * LANES + width, i * LANES : i * LANES + height] = h
            gram_low[j * LANES : j * LANES + width, i * LANES : i * LANES + height] = l

    def images(subspace):
        h, l = split(subspace)
        both = dot(gram_high[...], jnp.concatenate([h, l], axis=1))
        return both[:, :size] + both[:, size:] + dot(gram_low[...], h)

    basis[...] = start_ref[...]

    def step(_, carry):
        basis[...] = orthonormal(images(basis[...]))
        return carry

    lax.fori_loop(0, ITERS, step, 0)
    lane = lax.broadcasted_iota(jnp.int32, (1, size), 1)
    masked = basis[...] * jnp.where(lane < ranks_ref[0], 1.0, 0.0)
    h, l = split(masked)
    core = dot(h, xh_ref[...], 0, 0) + dot(h, xl_ref[...], 0, 0) + dot(l, xh_ref[...], 0, 0)
    parts, rows, _ = core_ref.shape
    for p in range(parts):
        core_ref[p] = core[p * rows : (p + 1) * rows, :]
    caught = jnp.sum(masked * images(masked), axis=0, keepdims=True)
    energy_ref[...] = caught / (trace / order)


def subspace_step(ranks, packed, start, x_high, x_low, parts):
    order, size = start.shape
    vmem = pl.BlockSpec(memory_space=pltpu.VMEM)
    return pl.pallas_call(
        subspace_kernel,
        in_specs=[pl.BlockSpec(memory_space=pltpu.SMEM)] + [vmem] * 4,
        out_specs=[vmem, vmem],
        out_shape=(
            jax.ShapeDtypeStruct((parts, size // parts, x_high.shape[1]), F32),
            jax.ShapeDtypeStruct((1, size), F32),
        ),
        scratch_shapes=[
            pltpu.VMEM((order, order), BF16),
            pltpu.VMEM((order, order), BF16),
            pltpu.VMEM((order, size), F32),
        ],
        compiler_params=pltpu.CompilerParams(vmem_limit_bytes=32 << 20),
        name="subspace",
    )(ranks, packed, start, x_high, x_low)


def arrange_kernel(slabs, blocks_ref, out_ref):
    for c in range(out_ref.shape[0]):
        pieces = [blocks_ref[s, :, c * slabs : (c + 1) * slabs] for s in range(blocks_ref.shape[0])]
        out_ref[c] = jnp.concatenate(pieces, axis=1)


def arrange(blocks, slabs, rows):
    parts, kept, _ = blocks.shape
    return pl.pallas_call(
        functools.partial(arrange_kernel, slabs),
        out_shape=jax.ShapeDtypeStruct((rows, kept, parts * slabs), F32),
        compiler_params=pltpu.CompilerParams(vmem_limit_bytes=32 << 20),
        name="arrange",
    )(blocks)


def shards(sizes, species_field, start_block, trunc_ranks):
    slabs, rows, order = species_field.shape
    packed = all_sum(gram_blocks(species_field), sizes)
    width = slabs * rows
    x_t = jnp.transpose(species_field, (2, 1, 0)).reshape(order, width)
    x_t = jnp.pad(x_t, ((0, 0), (0, -width % LANES)))
    rounded = lax.reduce_precision(x_t, 8, 7)
    x_high = rounded.astype(BF16)
    x_low = (x_t - rounded).astype(BF16)
    core, energies = subspace_step(trunc_ranks, packed, start_block, x_high, x_low, sizes[0])
    core = lax.all_to_all(core, "gx", split_axis=0, concat_axis=0, tiled=True)
    core = arrange(core, slabs, rows)
    return (jnp.transpose(core, (1, 0, 2)), energies[0])


def solution(mesh):
    sizes = (mesh.shape["gx"], mesh.shape["gy"])
    in_specs = (P("gx", "gy", None), P(), P())
    out_specs = (P("gx", "gy", None), P())
    return jax.shard_map(
        functools.partial(shards, sizes), mesh=mesh, in_specs=in_specs, out_specs=out_specs, check_vma=False
    )
```

```python
import functools

import jax
import jax.numpy as jnp
from jax import lax
from jax.experimental import pallas as pl
from jax.experimental.pallas import tpu as pltpu
from jax.sharding import PartitionSpec as P

ITERS = 3
LANES = 128
PANEL = 16
F32 = jnp.float32
BF16 = jnp.bfloat16


def split(value):
    high = value.astype(BF16)
    return high, (value - high.astype(F32)).astype(BF16)


def dot(left, right, left_dim=1, right_dim=0):
    return lax.dot_general(
        left, right, (((left_dim,), (right_dim,)), ((), ())), preferred_element_type=F32
    )


def packed_blocks(order):
    full, rest = divmod(order, LANES)
    blocks, row = {}, 0
    for i in range(full):
        for j in range(i, full):
            blocks[i, j] = row
            row += LANES
    if rest:
        for j in range(full + 1):
            blocks[full, j] = row
            row += rest
    return blocks, row


def pieces_of(first, count, piece):
    done = 0
    while done < count:
        index, at = divmod(first + done, piece)
        step = min(count - done, piece - at)
        yield index, at, done, step
        done += step


def piece_rows(order, parts):
    _, packed = packed_blocks(order)
    return -(-packed // (8 * parts)) * 8


def gram_kernel(me_ref, x_ref, out_ref, flat, high, low):
    slabs, rows, order = x_ref.shape
    parts, piece, _ = out_ref.shape
    pitch = -(-rows // 8) * 8
    for b in range(slabs):
        flat[pl.ds(b * pitch, rows), :] = x_ref[b]
        if pitch > rows:
            flat[pl.ds(b * pitch + rows, pitch - rows), :] = jnp.zeros((pitch - rows, order), F32)
    spare = flat.shape[0] - slabs * pitch
    if spare:
        flat[pl.ds(slabs * pitch, spare), :] = jnp.zeros((spare, order), F32)
    h, l = split(flat[...])
    high[...] = h
    low[...] = l
    full, rest = divmod(order, LANES)
    blocks, packed = packed_blocks(order)
    me = me_ref[0]

    def put(first, value):
        for index, at, begin, count in pieces_of(first, value.shape[0], piece):
            away = me ^ index
            slot = (away & 1) * (parts // 2) + (away >> 1)
            out_ref[slot, pl.ds(at, count), :] = value[begin : begin + count, :]

    for i in range(full):
        rows_i = slice(i * LANES, (i + 1) * LANES)
        cols = slice(i * LANES, full * LANES)
        product = (
            dot(high[:, rows_i], high[:, cols], 0, 0)
            + dot(high[:, rows_i], low[:, cols], 0, 0)
            + dot(low[:, rows_i], high[:, cols], 0, 0)
        )
        for j in range(i, full):
            put(blocks[i, j], product[:, (j - i) * LANES : (j - i + 1) * LANES])
    if rest:
        rows_i = slice(full * LANES, order)
        product = (
            dot(high[:, rows_i], high[...], 0, 0)
            + dot(high[:, rows_i], low[...], 0, 0)
            + dot(low[:, rows_i], high[...], 0, 0)
        )
        for j in range(full):
            put(blocks[full, j], product[:, j * LANES : (j + 1) * LANES])
        corner = product[:, full * LANES :]
        put(blocks[full, full], jnp.concatenate([corner, jnp.zeros((rest, LANES - rest), F32)], axis=1))
    if parts * piece > packed:
        put(packed, jnp.zeros((parts * piece - packed, LANES), F32))


def gram_pieces(me, x, parts):
    slabs, rows, order = x.shape
    depth = -(-slabs * (-(-rows // 8) * 8) // 16) * 16
    vmem = pl.BlockSpec(memory_space=pltpu.VMEM)
    return pl.pallas_call(
        gram_kernel,
        in_specs=[pl.BlockSpec(memory_space=pltpu.SMEM), vmem],
        out_specs=vmem,
        out_shape=jax.ShapeDtypeStruct((parts, piece_rows(order, parts), LANES), F32),
        scratch_shapes=[
            pltpu.VMEM((depth, order), F32),
            pltpu.VMEM((depth, order), BF16),
            pltpu.VMEM((depth, order), BF16),
        ],
        compiler_params=pltpu.CompilerParams(vmem_limit_bytes=32 << 20),
        name="gram",
    )(me, x)


def swap(value, sizes, flip_x, flip_y=(0, 0)):
    count_x, count_y = sizes
    pairs = []
    for i in range(count_x):
        for j in range(count_y):
            pairs.append((i * count_y + j, (i ^ flip_x[i & 1]) * count_y + (j ^ flip_y[i & 1])))
    return lax.ppermute(value, ("gx", "gy"), pairs)


def wide(block, column):
    return jnp.broadcast_to(block[:, column : column + 1], block.shape)


def total(terms):
    while len(terms) > 1:
        last = [terms[-1]] if len(terms) % 2 else []
        terms = [a + b for a, b in zip(terms[::2], terms[1::2])] + last
    return terms[0]


def inverse_factor(work, out):
    size = work.shape[0]
    lane = lax.broadcasted_iota(jnp.int32, (PANEL, size), 1)
    sub = lax.broadcasted_iota(jnp.int32, (PANEL, size), 0)
    lane8 = lax.broadcasted_iota(jnp.int32, (8, size), 1)
    for p in range(0, size, PANEL):
        rows = work[p : p + PANEL, :]
        cols = [wide(rows, p + k) for k in range(PANEL)]
        inside = (lane >= p) & (lane < p + PANEL)
        fwd = jnp.where(inside, jnp.where(lane == sub + p, 1.0, 0.0), rows)
        full = fwd
        inverse = jnp.zeros((PANEL, size), F32)
        for j in range(PANEL):
            pivot = 1.0 / cols[j][j : j + 1, :]
            inverse = jnp.where(sub == j, pivot, inverse)
            factor = cols[j] * pivot
            below = jnp.where(sub > j, factor, 0.0)
            other = jnp.where(sub == j, 0.0, factor)
            fwd = fwd - below * fwd[j : j + 1, :]
            full = full - other * full[j : j + 1, :]
            for k in range(j + 1, PANEL):
                cols[k] = cols[k] - other * cols[k][j : j + 1, :]
        out[p : p + PANEL, :] = jnp.where(lane <= sub + p, fwd * lax.sqrt(inverse), 0.0)
        full = full * inverse
        inside = (lane8 >= p) & (lane8 < p + PANEL)
        for b in range(p + PANEL, size, 8):
            block = work[b : b + 8, :]
            change = total([wide(block, p + k) * full[k : k + 1, :] for k in range(PANEL)])
            work[b : b + 8, :] = jnp.where(inside, 0.0, block) - change


def orthonormal(columns, work, inverse):
    size = columns.shape[1]
    i = lax.broadcasted_iota(jnp.int32, (size, size), 0)
    j = lax.broadcasted_iota(jnp.int32, (size, size), 1)
    both = jnp.concatenate(split(columns), axis=1)
    four = dot(both, both, 0, 0)
    cross_gram = four[:size, :size] + four[size:, size:] + (four[:size, size:] + four[size:, :size])
    diagonal = jnp.where(i == j, cross_gram, 0.0)
    scale_row = lax.rsqrt(jnp.sum(diagonal, axis=0, keepdims=True))
    scale_col = lax.rsqrt(jnp.sum(diagonal, axis=1, keepdims=True))
    work[...] = cross_gram * scale_row * scale_col
    inverse_factor(work, inverse)
    right = jnp.concatenate(split(inverse[...] * scale_row), axis=0)
    product = dot(both, jnp.concatenate([right, right], axis=1), 1, 1)
    return product[:, :size] + product[:, size:]


def subspace_kernel(
    me_ref, ranks_ref, own_ref, sibling_ref, start_ref, xh_ref, xl_ref,
    core_ref, energy_ref, packed, gram_high, gram_low, basis, work, inverse,
):
    order, size = start_ref.shape
    blocks, _ = packed_blocks(order)
    full, rest = divmod(order, LANES)
    parts, piece, _ = packed.shape
    me = me_ref[0]
    for away in range(parts):
        source = sibling_ref if away & 1 else own_ref
        packed[me ^ away] = source[away >> 1]

    trace = jnp.zeros((1, 1), F32)
    for (i, j), first in blocks.items():
        height = LANES if i < full else rest
        width = LANES if j < full else rest
        parted = [packed[index, at : at + count, :] for index, at, _, count in pieces_of(first, height, piece)]
        block = (jnp.concatenate(parted, axis=0) if len(parted) > 1 else parted[0])[:, :width]
        if i == j:
            a = lax.broadcasted_iota(jnp.int32, (height, width), 0)
            b = lax.broadcasted_iota(jnp.int32, (height, width), 1)
            trace = trace + jnp.sum(jnp.where(a == b, block, 0.0), keepdims=True)
        h, l = split(block)
        gram_high[i * LANES : i * LANES + height, j * LANES : j * LANES + width] = h
        gram_low[i * LANES : i * LANES + height, j * LANES : j * LANES + width] = l
        if i != j:
            h, l = split(block.T)
            gram_high[j * LANES : j * LANES + width, i * LANES : i * LANES + height] = h
            gram_low[j * LANES : j * LANES + width, i * LANES : i * LANES + height] = l

    def images(subspace):
        h, l = split(subspace)
        both = dot(gram_high[...], jnp.concatenate([h, l], axis=1))
        return both[:, :size] + both[:, size:] + dot(gram_low[...], h)

    basis[...] = start_ref[...]

    def step(_, carry):
        basis[...] = orthonormal(images(basis[...]), work, inverse)
        return carry

    lax.fori_loop(0, ITERS, step, 0)
    lane = lax.broadcasted_iota(jnp.int32, (1, size), 1)
    masked = basis[...] * jnp.where(lane < ranks_ref[0], 1.0, 0.0)
    h, l = split(masked)
    core = dot(h, xh_ref[...], 0, 0) + dot(h, xl_ref[...], 0, 0) + dot(l, xh_ref[...], 0, 0)
    kept = core_ref.shape[1]
    for p in range(parts):
        away = me ^ p
        core_ref[(away & 1) * (parts // 2) + (away >> 1)] = core[p * kept : (p + 1) * kept, :]
    caught = jnp.sum(masked * images(masked), axis=0, keepdims=True)
    energy_ref[...] = caught / (trace / order)


def subspace_step(me, ranks, own, sibling, start, x_high, x_low):
    order, size = start.shape
    parts, piece = 2 * own.shape[0], own.shape[1]
    vmem = pl.BlockSpec(memory_space=pltpu.VMEM)
    smem = pl.BlockSpec(memory_space=pltpu.SMEM)
    return pl.pallas_call(
        subspace_kernel,
        in_specs=[smem, smem] + [vmem] * 5,
        out_specs=[vmem, vmem],
        out_shape=(
            jax.ShapeDtypeStruct((parts, size // parts, x_high.shape[1]), F32),
            jax.ShapeDtypeStruct((1, size), F32),
        ),
        scratch_shapes=[
            pltpu.VMEM((parts, piece, LANES), F32),
            pltpu.VMEM((order, order), BF16),
            pltpu.VMEM((order, order), BF16),
            pltpu.VMEM((order, size), F32),
            pltpu.VMEM((size, size), F32),
            pltpu.VMEM((size, size), F32),
        ],
        compiler_params=pltpu.CompilerParams(vmem_limit_bytes=32 << 20),
        name="subspace",
    )(me, ranks, own, sibling, start, x_high, x_low)


def arrange_kernel(slabs, me_ref, *refs):
    *block_refs, out_ref, held = refs
    me = me_ref[0]
    for step, ref in enumerate(block_refs):
        for c in range(2):
            held[me ^ (2 * step + c)] = ref[c]
    for c in range(out_ref.shape[0]):
        out_ref[c] = jnp.concatenate(
            [held[s, :, c * slabs : (c + 1) * slabs] for s in range(held.shape[0])], axis=1
        )


def arrange(me, blocks, slabs, rows):
    _, kept, width = blocks[0].shape
    parts = 2 * len(blocks)
    vmem = pl.BlockSpec(memory_space=pltpu.VMEM)
    return pl.pallas_call(
        functools.partial(arrange_kernel, slabs),
        in_specs=[pl.BlockSpec(memory_space=pltpu.SMEM)] + [vmem] * len(blocks),
        out_specs=vmem,
        out_shape=jax.ShapeDtypeStruct((rows, kept, parts * slabs), F32),
        scratch_shapes=[pltpu.VMEM((parts, kept, width), F32)],
        compiler_params=pltpu.CompilerParams(vmem_limit_bytes=32 << 20),
        name="arrange",
    )(me, *blocks)


def shards(sizes, species_field, start_block, trunc_ranks):
    slabs, rows, order = species_field.shape
    count_x, count_y = sizes
    half = count_x // 2
    me = lax.axis_index("gx").astype(jnp.int32)[None]
    sibling = (1, 1)

    pieces = gram_pieces(me, species_field, count_x)
    arrived = swap(pieces[half:], sizes, sibling)
    flat = jnp.transpose(species_field, (1, 0, 2)).reshape(slabs * rows, order)
    partial = [pieces[t] + arrived[t] for t in range(half)]
    arrived = [swap(partial[t], sizes, (2 * t, 2 * t)) for t in range(1, half)]
    arrived, flat = lax.optimization_barrier((arrived, flat))
    value = total([partial[0]] + arrived)
    width = slabs * rows
    field = jnp.pad(flat.T, ((0, 0), (0, -width % LANES)))
    rounded = lax.reduce_precision(field, 8, 7)
    x_high = rounded.astype(BF16)
    x_low = (field - rounded).astype(BF16)
    bits = [1 << b for b in range(count_y.bit_length() - 1)]
    for step, flip in enumerate(zip(bits, reversed(bits))):
        other = swap(value, sizes, (0, 0), flip)
        if step == 0:
            other, x_high, x_low = lax.optimization_barrier((other, x_high, x_low))
        value = value + other
    own = jnp.stack([value] + [swap(value, sizes, (2 * t, 2 * t)) for t in range(1, half)])
    core, energies = subspace_step(
        me, trunc_ranks, own, swap(own, sizes, sibling), start_block, x_high, x_low
    )

    arrived = swap(core[half:], sizes, sibling)
    sends = [jnp.stack([core[t], arrived[t]]) for t in range(half)]
    blocks = [sends[0]] + [swap(sends[t], sizes, (2 * t, 2 * t)) for t in range(1, half)]
    core = arrange(me, blocks, slabs, rows)
    return (jnp.transpose(core, (1, 0, 2)), energies[0])


def solution(mesh):
    sizes = (mesh.shape["gx"], mesh.shape["gy"])
    in_specs = (P("gx", "gy", None), P(), P())
    out_specs = (P("gx", "gy", None), P())
    return jax.shard_map(
        functools.partial(shards, sizes), mesh=mesh, in_specs=in_specs, out_specs=out_specs, check_vma=False
    )
```
